32 devices in a mesh: pair: 8 (over z, x), col: 2 (over y), freq: 2 (over core).
Axes of the slice: x: 2, y: 2, z: 4, core: 2. Of those that a mesh axis runs over, the one named last changes fastest.
Arguments:
- pair_matrix: bfloat16 [24576, 2048], P('pair', 'col'), may hold values from -0.0546875 to 0.0546875
- energies: float32 [24576], P('pair'), may hold values from 0.5 to 20
- omega: float32 [2], P('freq'), may hold values from 0.2 to 10
Outputs:
- chi: float32 [2048, 2, 2048], P('pair', 'freq', 'col')
The draws below stay inside these ranges and needn't reach their ends.
All inputs are finite; a program needn't handle non-finite values.
Results may differ from the reference program's by a relative error of at most 0.00053.
Values may be sent and summed in bfloat16 or wider, within the bound.
No kernel may reach another device: no remote copies, remote signals or barrier semaphores. Data moves between devices by JAX's collectives and lax.ppermute only.
A program may use at most 128 MiB of HBM per device.

```python
import math
import jax
import jax.numpy as jnp
from jax import lax

K = 2048
NPAIR = 24576
NFREQ = 2


def strengthened(result, stream_key, source, target, shards_of, factor):
    def block_of(position):
        return (jnp.arange(result.shape[position]) // (result.shape[position] // shards_of)).reshape((-1,) + (1,) * (result.ndim - 1 - position))

    first = jax.random.permutation(stream_key, shards_of)[block_of(target)]
    far = (block_of(target) + shards_of // 2) % shards_of
    return jnp.where((block_of(source) == first) | (block_of(source) == far), factor * result, result)


def block_scale(rng, shape, pieces, low, top_value):
    loudness = 1.0
    for position, parts in pieces:
        steps = jax.random.uniform(jax.random.fold_in(jax.random.fold_in(rng, 6), position), (parts,), jnp.float32, low / len(pieces), top_value / len(pieces))
        loudness = loudness * jnp.repeat(jnp.exp(steps), shape[position] // parts).reshape((-1,) + (1,) * (len(shape) - 1 - position))
    return loudness


def noise_with(own_key, shape, deviation, bound, cuts, heavy, kind=jnp.bfloat16):
    result = deviation * jax.random.normal(own_key, shape, jnp.float32)
    if cuts:
        result = result * block_scale(own_key, shape, cuts, -0.22, 0.18)
    return jnp.clip(strengthened(result, jax.random.fold_in(own_key, 3), *heavy), -bound, bound).astype(kind)


def setup_inputs(seed: int = 0) -> dict:
    seeds = jax.random.split(jax.random.key(seed), 4)
    pair_matrix = noise_with(seeds[0], (NPAIR, K), NPAIR ** -0.5, 0.0546875, ((0, 8), (1, 2)), (0, 1, 8, 2.0))
    energies = jnp.clip(jnp.exp(math.log(20.0) - 3.6888795 * jax.random.uniform(seeds[1], (NPAIR,), jnp.float32) ** block_scale(seeds[1], (NPAIR,), ((0, 8),), -0.2, 0.2)), 0.5, 20.0)
    omega = jnp.clip(jnp.exp(math.log(10.0) - 3.912023 * jax.random.uniform(seeds[2], (NFREQ,), jnp.float32) ** block_scale(seeds[2], (NFREQ,), ((0, 2),), -0.2, 0.2)), 0.2, 10.0)
    return dict(pair_matrix=pair_matrix, energies=energies, omega=omega)


def reference(pair_matrix, energies, omega):
    width = math.gcd(NPAIR, 4096)
    count = NPAIR // width
    results = []
    for index in range(NFREQ):
        freq_value = omega[index]
        factor = jnp.sqrt(4.0 * energies / (energies * energies + freq_value * freq_value))

        def accumulate(total, block):
            begin = (block * width).astype(jnp.int32)
            rows = lax.dynamic_slice_in_dim(pair_matrix, begin, width, 0)
            scale = lax.dynamic_slice_in_dim(factor, begin, width, 0)
            rounded = (scale[:, None] * rows.astype(jnp.float32)).astype(jnp.bfloat16)
            rounded = lax.optimization_barrier(rounded).astype(jnp.float32)
            product = jnp.dot(rounded.T, rounded, precision=lax.Precision.HIGHEST)
            return (total - product, None)
        start = jnp.zeros((K, K), jnp.float32)
        total, unused = lax.scan(accumulate, start, jnp.arange(count, dtype=jnp.int32))
        results.append(total)
    return jnp.stack(results, axis=1)
```

```python
import jax
import jax.numpy as jnp
from jax import lax
from jax.sharding import PartitionSpec as P


WIRE = jnp.float16
LIMIT = 2.0**14


def build(mesh):
    npair = mesh.shape["pair"]
    bits = npair.bit_length() - 1
    stages = bits - 1
    last_pieces = 2

    def over_y(a):
        return lax.ppermute(a, "col", [(0, 1), (1, 0)])

    def over_core(a):
        return lax.ppermute(a, "freq", [(0, 1), (1, 0)])

    def over_bit(a, b):
        return lax.ppermute(a, "pair", [(p, p ^ (1 << b)) for p in range(npair)])

    def over_top(a, parity):
        top = npair // 2
        moves = [
            (2 * p + y, 2 * (p ^ top) + y)
            for p in range(npair)
            for y in range(2)
            if (p // top) ^ y == parity
        ]
        return lax.ppermute(a, ("pair", "col"), moves)

    def per_device(raw, energies, omega):
        pairs, cols = raw.shape
        half = pairs // 2
        rows = 2 * cols // npair
        me = lax.axis_index("pair")
        y = lax.axis_index("col")
        f = lax.axis_index("freq")

        def bit(b):
            return (me >> b) & 1

        factor = jnp.sqrt(4.0 * energies / (energies * energies + omega[0] * omega[0]))
        first = lax.dynamic_slice_in_dim(factor, f * half, half)
        second = lax.dynamic_slice_in_dim(factor, (1 - f) * half, half)
        factors = jnp.concatenate([first, second])[:, None]

        def scaled(a):
            return (factors * a.astype(jnp.float32)).astype(jnp.bfloat16)

        def block_ids(b):
            if b == stages:
                return [me & ((1 << b) - 1)]
            low = (me & ((1 << (b + 1)) - 1)) ^ (1 << b)
            return [low + (t << (b + 1)) for t in range(1 << (stages - 1 - b))]

        def columns(a, ids):
            return [lax.dynamic_slice_in_dim(a, i * rows, rows, 1) for i in ids]

        mine = lax.dynamic_slice_in_dim(raw, f * half, half, 0)
        pieces = []
        for b in range(stages + 1):
            for part in columns(mine, block_ids(b)):
                if b < stages:
                    pieces.append((b, part))
                else:
                    width = rows // last_pieces
                    for k in range(last_pieces):
                        pieces.append((b, part[:, k * width : (k + 1) * width]))
        arrived = []
        for b, part in pieces:
            got = over_y(part)
            arrived.append((b, jnp.concatenate([got, over_core(got)], 0)))

        rolled = jnp.concatenate(
            [mine, lax.dynamic_slice_in_dim(raw, (1 - f) * half, half, 0)], 0
        )
        own = scaled(rolled)

        bound = jnp.max(jnp.abs(raw)).astype(jnp.float32) * jnp.max(factor)
        bound = jnp.full((8, 128), bound, jnp.float32)
        bound = jnp.maximum(bound, over_y(bound))
        for b in range(bits):
            bound = jnp.maximum(bound, over_bit(bound, b))
        bound = jnp.maximum(bound[0, 0], 1e-18)
        total = float(npair * pairs) * bound * bound
        down = LIMIT / total
        up = total / LIMIT

        def wire(a):
            return (a * down).astype(WIRE)

        def unwire(a):
            return a.astype(jnp.float32) * up

        def gram(left):
            return -lax.dot_general(
                left, own, (((0,), (0,)), ((), ())), preferred_element_type=jnp.float32
            )

        def reduce(parts, parity):
            received = []
            for b in range(stages):
                value = jnp.concatenate(parts[b], 0)
                value = value.reshape(-1, rows, value.shape[-1])
                for got in received_at(received, b):
                    value = value + unwire(got)
                received.append(over_bit(wire(value), b))
            start = 0
            out = []
            for part in parts[stages]:
                stop = start + part.shape[0]
                value = part
                for got in received_at(received, stages):
                    value = value + unwire(got[0, start:stop])
                out.append((value, over_top(wire(value), parity)))
                start = stop
            return out

        def received_at(received, b):
            picked = []
            for s, got in enumerate(received):
                for c in range(s + 1, b + 1):
                    want = bit(c) if c < b or b == stages else 1 - bit(c)
                    if c == stages:
                        break
                    got = got.reshape((got.shape[0] // 2, 2) + got.shape[1:])
                    got = lax.dynamic_index_in_dim(got, want, 1, keepdims=False)
                picked.append(got)
            return picked

        diagonal = reduce(
            [[gram(c) for c in columns(own, block_ids(b))] for b in range(stages + 1)], 1
        )
        parts = [[] for _ in range(stages + 1)]
        for b, part in arrived:
            parts[b].append(gram(scaled(part)))
        crossed = reduce(parts, 0)

        here = (me // (npair // 2)) == y
        kept, sent = diagonal[0]
        width = rows // last_pieces
        out = []
        for k, (value, got) in enumerate(crossed):
            cut = slice(k * width, (k + 1) * width)
            out.append(
                jnp.where(here, kept[cut], value) + unwire(sent[cut]) + unwire(got)
            )
        return jnp.concatenate(out, 0)[:, None, :]

    return per_device


def solution(mesh):
    return jax.shard_map(
        build(mesh),
        mesh=mesh,
        in_specs=(P("pair", "col"), P("pair"), P("freq")),
        out_specs=P("pair", "freq", "col"),
        check_vma=False,
    )
```

```python
import jax
import jax.numpy as jnp
from jax import lax
from jax.sharding import PartitionSpec as P


WIRE = jnp.float16
LIMIT = 2.0**14


def build(mesh):
    npair = mesh.shape["pair"]
    bits = npair.bit_length() - 1
    stages = bits - 1

    def over_y(a):
        return lax.ppermute(a, "col", [(0, 1), (1, 0)])

    def over_core(a):
        return lax.ppermute(a, "freq", [(0, 1), (1, 0)])

    def over_bit(a, b):
        return lax.ppermute(a, "pair", [(p, p ^ (1 << b)) for p in range(npair)])

    def over_top(a, parity):
        top = npair // 2
        moves = [
            (2 * p + y, 2 * (p ^ top) + y)
            for p in range(npair)
            for y in range(2)
            if (p // top) ^ y == parity
        ]
        return lax.ppermute(a, ("pair", "col"), moves)

    def per_device(raw, energies, omega):
        pairs, cols = raw.shape
        half = pairs // 2
        blocks = npair // 2
        rows = cols // blocks
        me = lax.axis_index("pair")
        y = lax.axis_index("col")
        f = lax.axis_index("freq")
        fine = stages == 2 and rows % 256 == 0
        widths = (rows // 2, rows // 2) if fine else (rows,)

        def bit(b):
            return lax.bitwise_and(lax.shift_right_logical(me, b), 1)

        def sending():
            return [2 * t + 1 - bit(0) for t in range(blocks // 2)]

        def keeping():
            return [2 * t + bit(0) for t in range(blocks // 2)]

        def piece(a, ids, start, width):
            mine = lax.dynamic_slice_in_dim(a, f * half, half, 0)
            parts = [
                lax.dynamic_slice_in_dim(mine, i * rows + start, width, 1) for i in ids
            ]
            return jnp.stack(parts)

        first = piece(raw, sending(), 0, widths[0])
        raw, first = lax.optimization_barrier((raw, first))
        arrivals = [over_y(first)]

        factor = jnp.sqrt(
            4.0 * energies / (energies * energies + omega[0] * omega[0])
        )[:, None]
        own = (factor * raw.astype(jnp.float32)).astype(jnp.bfloat16)
        bound = jnp.max(jnp.abs(own).astype(jnp.float32), 0, keepdims=True)
        bound = lax.optimization_barrier(bound)
        bound = jnp.full((8, 128), jnp.max(bound), jnp.float32)
        for b in range(bits):
            bound = jnp.maximum(bound, over_bit(bound, b))
        other = over_y(bound)

        def links(bound_):
            total = jnp.maximum(float(npair * pairs) * bound_[0, 0], 1e-30)
            return LIMIT / total, total / LIMIT

        if fine:
            zz = bit(1)
            away, stay = 2 * (1 - zz) + bit(0), 2 * zz + bit(0)
            w = widths[0]
            pieces = [
                piece(raw, sending(), w, w),
                piece(raw, [away, stay], 0, w),
                piece(raw, [away], w, w),
                piece(raw, [stay], w, w),
            ]
        else:
            pieces = [piece(raw, keeping(), 0, rows)]
        for part in pieces:
            arrivals.append(over_y(part))
        lefts = []
        for got in arrivals:
            lefts.append((got, over_core(got)))

        def wire(a, scale):
            return (a * scale[0]).astype(WIRE)

        def unwire(a, scale):
            return a.astype(jnp.float32) * scale[1]

        def gram(left):
            return -lax.dot_general(
                left, own, (((0,), (0,)), ((), ())), preferred_element_type=jnp.float32
            )

        def cross(pair, token):
            near, far, token = lax.optimization_barrier((*pair, token))
            low = jnp.where(f == 0, near, far)
            high = jnp.where(f == 0, far, near)
            left = jnp.concatenate(
                [jnp.concatenate([low[t], high[t]], 0) for t in range(near.shape[0])], 1
            )
            value = gram((factor * left.astype(jnp.float32)).astype(jnp.bfloat16))
            return value.reshape(near.shape[0], near.shape[2], cols)

        def pick(value, b, which):
            value = value.reshape((value.shape[0] // 2, 2) + value.shape[1:])
            index = bit(b) if which else 1 - bit(b)
            return lax.dynamic_index_in_dim(value, index, 1, keepdims=False)

        def hop(b, value, scale):
            return over_bit(wire(value, scale), b)

        def finish(value, scale, parity):
            value = value.reshape(value.shape[-2:])
            return value, over_top(wire(value, scale), parity)

        inner = links(bound * bound)
        outer = links(bound * other)

        value = lax.optimization_barrier(gram(own)).reshape(blocks, rows, cols)
        token = value
        for b in reversed(range(stages)):
            value = value.reshape(2, 1 << b, rows, cols)
            send = lax.dynamic_index_in_dim(value, 1 - bit(b), 0, keepdims=False)
            got = hop(b, send, inner)
            value = lax.dynamic_index_in_dim(value, bit(b), 0, keepdims=False)
            value = value + unwire(got, inner)
        kept, sent = finish(value, inner, 1)

        crossed = []
        if fine:
            send0 = cross(lefts[0], token)
            got0 = hop(0, send0, outer)
            send1 = cross(lefts[1], send0)
            got1 = hop(0, send1, outer)
            keep0 = lax.optimization_barrier(cross(lefts[2], send1))
            value = keep0[0] + unwire(pick(got0, 1, False)[0], outer)
            got = hop(1, value, outer)
            value = keep0[1] + unwire(pick(got0, 1, True)[0], outer)
            value = value + unwire(got, outer)
            crossed.append(finish(value, outer, 0))
            away1 = cross(lefts[3], keep0)
            value = away1[0] + unwire(pick(got1, 1, False)[0], outer)
            got = hop(1, value, outer)
            stay1 = cross(lefts[4], away1)
            value = stay1[0] + unwire(pick(got1, 1, True)[0], outer)
            value = value + unwire(got, outer)
            crossed.append(finish(value, outer, 0))
        else:
            send = cross(lefts[0], token)
            got = hop(0, send, outer)
            value = cross(lefts[1], send) + unwire(got, outer)
            for b in range(1, stages):
                got = hop(b, pick(value, b, False), outer)
                value = pick(value, b, True) + unwire(got, outer)
            crossed.append(finish(value, outer, 0))

        here = lax.shift_right_logical(me, stages) == y
        out = []
        start = 0
        for value, got in crossed:
            cut = slice(start, start + value.shape[0])
            out.append(
                jnp.where(here, kept[cut], value)
                + unwire(sent[cut], inner)
                + unwire(got, outer)
            )
            start += value.shape[0]
        return jnp.concatenate(out, 0)[:, None, :]

    return per_device


def solution(mesh):
    return jax.shard_map(
        build(mesh),
        mesh=mesh,
        in_specs=(P("pair", "col"), P("pair"), P("freq")),
        out_specs=P("pair", "freq", "col"),
        check_vma=False,
    )
```

```python
import jax
import jax.numpy as jnp
from jax import lax
from jax.sharding import PartitionSpec as P


WIRE = jnp.float16
LIMIT = 2.0**14


def build(mesh):
    npair = mesh.shape["pair"]
    bits = npair.bit_length() - 1
    stages = bits - 1

    def over_y(a):
        return lax.ppermute(a, "col", [(0, 1), (1, 0)])

    def over_core(a):
        return lax.ppermute(a, "freq", [(0, 1), (1, 0)])

    def over_bit(a, b):
        return lax.ppermute(a, "pair", [(p, p ^ (1 << b)) for p in range(npair)])

    def over_top(a, parity):
        top = npair // 2
        moves = [
            (2 * p + y, 2 * (p ^ top) + y)
            for p in range(npair)
            for y in range(2)
            if (p // top) ^ y == parity
        ]
        return lax.ppermute(a, ("pair", "col"), moves)

    def per_device(raw, energies, omega):
        pairs, cols = raw.shape
        half = pairs // 2
        blocks = npair // 2
        rows = cols // blocks
        me = lax.axis_index("pair")
        y = lax.axis_index("col")
        f = lax.axis_index("freq")
        fine = stages == 2 and rows % 256 == 0
        widths = (rows // 2, rows // 2) if fine else (rows,)

        def bit(b):
            return lax.bitwise_and(lax.shift_right_logical(me, b), 1)

        def sending():
            return [2 * t + 1 - bit(0) for t in range(blocks // 2)]

        def keeping():
            return [2 * t + bit(0) for t in range(blocks // 2)]

        def piece(a, ids, start, width):
            mine = lax.dynamic_slice_in_dim(a, f * half, half, 0)
            parts = [
                lax.dynamic_slice_in_dim(mine, i * rows + start, width, 1) for i in ids
            ]
            return jnp.stack(parts)

        first = piece(raw, sending(), 0, widths[0])
        raw, first = lax.optimization_barrier((raw, first))
        arrivals = [over_y(first)]

        factor = jnp.sqrt(
            4.0 * energies / (energies * energies + omega[0] * omega[0])
        )[:, None]
        own = (factor * raw.astype(jnp.float32)).astype(jnp.bfloat16)
        bound = jnp.max(jnp.abs(own).astype(jnp.float32), 0, keepdims=True)
        bound = lax.optimization_barrier(bound)
        bound = jnp.full((8, 128), jnp.max(bound), jnp.float32)
        for b in range(bits):
            bound = jnp.maximum(bound, over_bit(bound, b))
        other = over_y(bound)

        def links(bound_):
            total = jnp.maximum(float(npair * pairs) * bound_[0, 0], 1e-30)
            return LIMIT / total, total / LIMIT

        if fine:
            zz = bit(1)
            away, stay = 2 * (1 - zz) + bit(0), 2 * zz + bit(0)
            w = widths[0]
            pieces = [
                piece(raw, sending(), w, w),
                piece(raw, [away, stay], 0, w),
                piece(raw, [away], w, w),
                piece(raw, [stay], w, w),
            ]
        else:
            pieces = [piece(raw, keeping(), 0, rows)]
        for part in pieces:
            arrivals.append(over_y(part))
        lefts = []
        for got in arrivals:
            lefts.append((got, over_core(got)))

        def wire(a, scale):
            return (a * scale[0]).astype(WIRE)

        def unwire(a, scale):
            return a.astype(jnp.float32) * scale[1]

        def gram(left):
            return -lax.dot_general(
                left, own, (((0,), (0,)), ((), ())), preferred_element_type=jnp.float32
            )

        def cross(pair, token):
            near, far, token = lax.optimization_barrier((*pair, token))
            low = jnp.where(f == 0, near, far)
            high = jnp.where(f == 0, far, near)
            left = jnp.concatenate(
                [jnp.concatenate([low[t], high[t]], 0) for t in range(near.shape[0])], 1
            )
            value = gram((factor * left.astype(jnp.float32)).astype(jnp.bfloat16))
            return value.reshape(near.shape[0], near.shape[2], cols)

        def pick(value, b, which):
            value = value.reshape((value.shape[0] // 2, 2) + value.shape[1:])
            index = bit(b) if which else 1 - bit(b)
            return lax.dynamic_index_in_dim(value, index, 1, keepdims=False)

        def hop(b, value, scale):
            return over_bit(wire(value, scale), b)

        def finish(value, scale, parity):
            value = value.reshape(value.shape[-2:])
            return value, over_top(wire(value, scale), parity)

        inner = links(bound * bound)
        outer = links(bound * other)

        high = bit(stages - 1) * (cols // 2)
        send = gram(lax.dynamic_slice_in_dim(own, cols // 2 - high, cols // 2, 1))
        send = lax.optimization_barrier(send)
        got = hop(stages - 1, send.reshape(-1, rows, cols), inner)
        value = gram(lax.dynamic_slice_in_dim(own, high, cols // 2, 1))
        value = lax.optimization_barrier(value).reshape(-1, rows, cols)
        token = bound
        for b in reversed(range(stages)):
            if b < stages - 1:
                value = value.reshape(2, 1 << b, rows, cols)
                send = lax.dynamic_index_in_dim(value, 1 - bit(b), 0, keepdims=False)
                got = hop(b, send, inner)
                value = lax.dynamic_index_in_dim(value, bit(b), 0, keepdims=False)
            value = value + unwire(got, inner)
        kept, sent = finish(value, inner, 1)

        crossed = []
        if fine:
            send0 = cross(lefts[0], token)
            got0 = hop(0, send0, outer)
            send1 = cross(lefts[1], send0)
            got1 = hop(0, send1, outer)
            keep0 = lax.optimization_barrier(cross(lefts[2], send1))
            value = keep0[0] + unwire(pick(got0, 1, False)[0], outer)
            got = hop(1, value, outer)
            value = keep0[1] + unwire(pick(got0, 1, True)[0], outer)
            value = value + unwire(got, outer)
            crossed.append(finish(value, outer, 0))
            away1 = cross(lefts[3], keep0)
            value = away1[0] + unwire(pick(got1, 1, False)[0], outer)
            got = hop(1, value, outer)
            stay1 = cross(lefts[4], away1)
            value = stay1[0] + unwire(pick(got1, 1, True)[0], outer)
            value = value + unwire(got, outer)
            crossed.append(finish(value, outer, 0))
        else:
            send = cross(lefts[0], token)
            got = hop(0, send, outer)
            value = cross(lefts[1], send) + unwire(got, outer)
            for b in range(1, stages):
                got = hop(b, pick(value, b, False), outer)
                value = pick(value, b, True) + unwire(got, outer)
            crossed.append(finish(value, outer, 0))

        here = lax.shift_right_logical(me, stages) == y
        out = []
        start = 0
        for value, got in crossed:
            cut = slice(start, start + value.shape[0])
            out.append(
                jnp.where(here, kept[cut], value)
                + unwire(sent[cut], inner)
                + unwire(got, outer)
            )
            start += value.shape[0]
        return jnp.concatenate(out, 0)[:, None, :]

    return per_device


def solution(mesh):
    return jax.shard_map(
        build(mesh),
        mesh=mesh,
        in_specs=(P("pair", "col"), P("pair"), P("freq")),
        out_specs=P("pair", "freq", "col"),
        check_vma=False,
    )
```
